128 devices in a mesh: stream: 16 (over y, z), rows: 8 (over x, core).
Axes of the slice: x: 4, y: 4, z: 4, core: 2. Of those that a mesh axis runs over, the one named last changes fastest.
Arguments:
- tracers: float32 [8, 512, 16384], P(None, 'rows', 'stream'), may hold values from -6 to 6
- shifts: int32 [512, 16384], P('rows', 'stream'), may hold values from 0 to 2046, as said below
- fractions: float32 [512, 16384], P('rows', 'stream'), may hold values from 0 to 1
- record_owner: int32 [8, 256, 1], P('rows', 'stream'), may hold values from 0 to 15; in each aligned block of 16 rows (0 to 15, 16 to 31, ..., all dimensions but the last counted through in order) at most 2 rows name the same one
- record_source: int32 [8, 256], P('rows', 'stream'), may hold values from 0 to 15
- record_parity: int32 [8, 256], P('rows', 'stream'), may hold values from 0 to 1
- record_place: int32 [8, 256], P('rows', 'stream'), may hold values from 0 to 31
Outputs:
- tracers_out: float32 [8, 512, 16384], P(None, 'rows', 'stream')
The draws below stay inside these ranges and needn't reach their ends.
Inputs may be any that keep to these rules, and one draw needn't show every extreme that they name: Along one row the shifts lie within five consecutive values; the largest is reached in every draw. `record_owner`: among the 16 records of one device at most 2 name the same owner.
All inputs are finite; a program needn't handle non-finite values.
Results may differ from the reference program's by a relative error of at most 0.0003.
Values sent between devices are 32-bit elements; how exact they have to be, the bound alone decides.
A program may use at most 128 MiB of HBM per device.

```python
import math
import jax
import jax.numpy as jnp
import numpy as np
from jax import lax

TRACERS = 8
BLOCK = 64
XD = 1024
SPAN = 2
CAP = 2
RECS = 16
NY = 512
NX = 16384
NREC = 256
N_STREAM = 16
N_ROWS = 8


def draw_shifts(key, part):
    largest = SPAN * XD - 2
    key_base, key_jitter, key_row, key_col = jax.random.split(key, 4)
    base_shift = jax.random.randint(key_base, (NY, 1), 0, largest - 3, dtype=jnp.int32)
    jitter = jax.random.randint(key_jitter, (NY, NX), 0, 5, dtype=jnp.int32)
    chosen_row = jax.random.randint(key_row, (), 0, NY, dtype=jnp.int32)
    chosen_col = jax.random.randint(key_col, (), 0, NX, dtype=jnp.int32)
    base_shift = base_shift.at[chosen_row, 0].set(largest - 4)
    jitter = jitter.at[chosen_row, chosen_col].set(4)
    return base_shift + jitter


def touch_ends(values, key, smallest, top_value):
    place = [jax.random.randint(jax.random.fold_in(key, axis), (), 0, length) for axis, length in enumerate(values.shape)]
    main_axis = values.shape.index(max(values.shape))
    next_to = place[:main_axis] + [(place[main_axis] + 1) % values.shape[main_axis]] + place[main_axis + 1:]
    return values.at[tuple(place)].set(smallest).at[tuple(next_to)].set(top_value)


def level_of(own_key, dims, cuts, low, high):
    gain = 1.0
    for position, shards_of in cuts:
        steps = jax.random.uniform(jax.random.fold_in(jax.random.fold_in(own_key, 6), position), (shards_of,), jnp.float32, low / len(cuts), high / len(cuts))
        gain = gain * jnp.repeat(jnp.exp(steps), dims[position] // shards_of).reshape((-1,) + (1,) * (len(dims) - 1 - position))
    return gain


def assign_block(key, own, number, rows, amount, top, limit, skew):
    order = jax.random.permutation(key, amount)
    crowded, ordinary = portions_of(amount, rows * top, limit, skew, True), portions_of(amount, rows * top, limit, skew, False)
    places = jnp.arange(amount)

    def named(tallies, turn):
        used = int((tallies > 0).sum())
        fixed = max(1, used // 4)
        shifted = fixed + (places - fixed + turn * (used - fixed)) % max(1, amount - fixed)
        return jnp.zeros((amount,), jnp.int32).at[order[jnp.where(places < fixed, places, shifted)]].set(jnp.asarray(tallies, jnp.int32))

    tallies = jnp.where(number % 4 == 0, named(crowded, number // 4), named(ordinary, number - number // 4 - 1))
    mixed = jax.random.permutation(jax.random.fold_in(own, 3), amount)
    donor, receiver = mixed[0:amount // 2 * 2:2], mixed[1:amount // 2 * 2:2]
    slack = jnp.minimum(tallies[donor] - 1, limit - tallies[receiver]) // 2
    slack = jnp.where((donor == order[0]) | (receiver == order[0]) | (tallies[receiver] == 0), 0, jnp.maximum(slack, 0))
    shifted = jax.random.randint(jax.random.fold_in(own, 4), (amount // 2,), 0, 1 << 20) % (slack + 1)
    tallies = tallies.at[donor].add(-shifted).at[receiver].add(shifted)
    labels = jnp.searchsorted(jnp.cumsum(tallies), jnp.arange(rows * top), side="right").astype(jnp.int32)
    listing = labels.reshape(top, rows).T
    listing = listing[jax.random.permutation(jax.random.fold_in(own, 1), rows)]
    turn = jax.random.randint(jax.random.fold_in(own, 2), (rows, 1), 0, top)
    return jnp.take_along_axis(listing, (jnp.arange(top)[None, :] + turn) % top, axis=1)


def portions_of(number_of, total, bound, skew, full):
    portions = [(1 << 20) // math.isqrt(standing ** skew) + 1 for standing in range(1, number_of + 1)]
    largest = bound if full else min(bound, max(-(-total // number_of), total * portions[0] // sum(portions)))
    least = 1 if total - largest >= number_of - 1 else 0
    counts, surplus = [largest] + [least] * (number_of - 1), total - largest - least * (number_of - 1)
    while surplus > 0:
        free = [i for i in range(1, number_of) if counts[i] < largest] or [i for i in range(1, number_of) if counts[i] < bound]
        whole, remaining = sum([portions[i] for i in free]), surplus
        for i in free:
            more = min(bound - counts[i], max(1, remaining * portions[i] // whole), surplus)
            counts[i] = counts[i] + more
            surplus = surplus - more
    return np.array(counts)


def centred(rng, dims, spread, bound, shards=(), held_as=jnp.bfloat16):
    drawn = jax.random.normal(rng, dims, jnp.float32) * spread
    if len(shards) > 0:
        drawn = level_of(rng, dims, shards, -0.22, 0.18) * drawn
    return jnp.clip(drawn, min=-bound, max=bound).astype(held_as)


def setup_inputs(seed: int = 0) -> dict:
    splits = jax.random.split(jax.random.key(seed), 8)
    tracers = centred(splits[0], (TRACERS, NY, NX), 1.0, 6.0, ((1, 8), (2, 16)), jnp.float32)
    shifts = draw_shifts(jax.random.fold_in(splits[7], 71), 0)
    fractions = jnp.clip(1.0 * jax.random.uniform(splits[2], (NY, NX), jnp.float32) ** level_of(splits[2], (NY, NX), ((0, 8), (1, 16)), -0.2, 0.2), 0.0, 1.0)
    record_owner_keys = jax.random.split(jax.random.fold_in(splits[3], 1), N_ROWS * NREC // RECS)
    record_owner_turns = jax.random.permutation(jax.random.fold_in(splits[3], 3), N_ROWS * NREC // RECS)
    record_owner = jax.vmap(lambda own, number: assign_block(jax.random.fold_in(splits[3], 2), own, number, RECS, N_STREAM, 1, CAP, 2))(record_owner_keys, record_owner_turns).reshape((N_ROWS, NREC, 1))
    record_source = touch_ends(jax.random.randint(splits[4], (N_ROWS, NREC), 0, XD // BLOCK), jax.random.fold_in(splits[4], 1), 0, (XD // BLOCK) - 1).astype(jnp.int32)
    record_parity = touch_ends(jax.random.randint(splits[5], (N_ROWS, NREC), 0, 2), jax.random.fold_in(splits[5], 1), 0, 1).astype(jnp.int32)
    record_place = touch_ends(jax.random.randint(splits[6], (N_ROWS, NREC), 0, 2 * XD // BLOCK), jax.random.fold_in(splits[6], 1), 0, (2 * XD // BLOCK) - 1).astype(jnp.int32)
    return {"tracers": tracers, "shifts": shifts, "fractions": fractions, "record_owner": record_owner, "record_source": record_source, "record_parity": record_parity, "record_place": record_place}


def reference(tracers, shifts, fractions, record_owner, record_source, record_parity, record_place):
    reach = SPAN * XD
    column = jnp.arange(NX, dtype=jnp.int32)[None, :]
    departure = (column - shifts + reach).astype(jnp.int32)

    def sweep_tracer(field):
        padded = jnp.concatenate([jnp.zeros((NY, reach), field.dtype), field], axis=1)
        prefix = jnp.cumsum(padded, axis=1)
        previous = jnp.concatenate([jnp.zeros((NY, 1), field.dtype), padded[:, :-1]], axis=1)
        slope = padded - previous
        whole_cells = prefix[:, reach:] - jnp.take_along_axis(prefix, departure, axis=1)
        upwind = jnp.take_along_axis(padded, departure, axis=1)
        upslope = jnp.take_along_axis(slope, departure, axis=1)
        face_flux = whole_cells + fractions * upwind + upslope * fractions * (1.0 - fractions) * 0.5
        left_flux = jnp.concatenate([jnp.zeros((NY, 1), field.dtype), face_flux[:, :-1]], axis=1)
        return face_flux, left_flux

    face_flux, left_flux = lax.map(sweep_tracer, tracers)
    advected = tracers + left_flux - face_flux

    half_rows = BLOCK // 2
    full_shape = (N_ROWS, NREC, half_rows)
    offsets = jnp.arange(half_rows, dtype=jnp.int32)
    row_group = jnp.arange(N_ROWS, dtype=jnp.int32)[:, None]
    stream_of = jnp.arange(NREC, dtype=jnp.int32)[None, :] // RECS
    source_col = (stream_of * XD + (record_source + 1) * BLOCK - 1).astype(jnp.int32)
    source_row = jnp.broadcast_to((row_group * BLOCK)[:, :, None] + 2 * offsets[None, None, :], full_shape).astype(jnp.int32)
    source_col3 = jnp.broadcast_to(source_col[:, :, None], full_shape).astype(jnp.int32)
    fine_flux = 0.5 * (face_flux[:, source_row, source_col3] + face_flux[:, source_row + 1, source_col3])
    target_base = (row_group - row_group % 2 + record_parity) * BLOCK + (record_place % 2) * half_rows
    target_col = record_owner[:, :, 0] * XD + (record_place // 2) * BLOCK
    target_row = jnp.broadcast_to(target_base[:, :, None] + offsets[None, None, :], full_shape).astype(jnp.int32)
    target_col3 = jnp.broadcast_to(target_col[:, :, None], full_shape).astype(jnp.int32)
    correction = 0.5 * (fine_flux - left_flux[:, target_row, target_col3])
    return advected.at[:, target_row, target_col3].add(correction)
```

```python
import jax
import jax.numpy as jnp
from jax import lax
from jax.experimental import pallas as pl
from jax.experimental.pallas import tpu as pltpu
from jax.sharding import PartitionSpec as P

BLOCK = 64
ROWS = 64
COLS = 1024
TR = 8
LANES = 128
TILES = COLS // LANES
PAD = 2
OWN = PAD + 2 * TILES
WIDTH = OWN + TILES + 1
CHUNKS = 8
CR = ROWS // CHUNKS
FORWARD = 5
MESH = pl.DeviceIdType.MESH
HIGHEST = lax.Precision.HIGHEST


def shifted(pieces, amount):
    if amount == 0:
        return pieces[:-1]
    lane = lax.broadcasted_iota(jnp.int32, (TR, LANES), 1)
    turned = [pltpu.roll(piece, LANES - amount, 1) for piece in pieces]
    return [
        jnp.where(lane < LANES - amount, turned[i], turned[i + 1]) for i in range(len(pieces) - 1)
    ]


def sweep_kernel(
    t_ref, shift_ref, frac_ref, owner_in, source_in, parity_in, place_in,
    out_ref,
    owner_ref, source_ref, parity_ref, place_ref, own_buf, near_buf, far_buf, work, relay_buf, shift_tile, frac_tile, least_v, least_s, lhs, ones_mat, faces,
    hot_a, hot_b, codes, send_buf, recv_buf,
    own_sem, tile_sem, record_sem, edge_send, edge_recv, least_sem,
    first_send, first_recv, middle_send, middle_recv, last_send, last_recv, msg_send, msg_recv, msg_own,
):
    s = lax.axis_index("stream")
    row = lax.axis_index("rows")
    y, z = s // 4, s % 4
    partner = row + 1 - 2 * (row % 2)
    after = ((s + 1) % 16, row)
    ahead = ((s + 15) % 16, row)
    via = (((y + jnp.where(z == 2, 1, 0)) % 4) * 4 + (z + 3) % 4, row)
    from_z = (z + 1) % 4
    from_s = ((y + jnp.where(from_z == 2, 3, 0)) % 4) * 4 + from_z
    relayed_to = ((from_s + 2) % 16, row)

    barrier = pltpu.get_barrier_semaphore()

    def greet(step, carry):
        other = (s + step) % 16
        pl.semaphore_signal(barrier, inc=1, device_id=(other, row), device_id_type=MESH)
        pl.semaphore_signal(barrier, inc=1, device_id=(other, partner), device_id_type=MESH)
        return carry

    lax.fori_loop(1, 16, greet, 0)
    pl.semaphore_signal(barrier, inc=1, device_id=(s, partner), device_id_type=MESH)
    own_copy = pltpu.make_async_copy(t_ref, own_buf, own_sem)
    own_copy.start()
    staged = [
        pltpu.make_async_copy(source, target, record_sem.at[i])
        for i, (source, target) in enumerate(
            [(owner_in, owner_ref), (source_in, source_ref), (parity_in, parity_ref), (place_in, place_ref)])
    ] + [
        pltpu.make_async_copy(source.at[:, pl.ds(j * LANES, LANES)], target.at[j + 1], tile_sem.at[i, j])
        for i, (source, target) in enumerate([(shift_ref, shift_tile), (frac_ref, frac_tile)])
        for j in range(TILES)
    ]
    for copy in staged:
        copy.start()
    pl.semaphore_wait(barrier, 31)

    def unit(ref, c):
        return ref.at[:, c]

    def direct(c):
        return pltpu.make_async_remote_copy(
            unit(t_ref, c), unit(near_buf, c),
            first_send.at[c], first_recv.at[c], device_id=after, device_id_type=MESH)

    def forward(c):
        return pltpu.make_async_remote_copy(
            unit(near_buf, c), unit(far_buf, c),
            last_send.at[c], last_recv.at[c], device_id=after, device_id_type=MESH)

    def leg_1(c):
        return pltpu.make_async_remote_copy(
            unit(t_ref, c), unit(relay_buf, c - FORWARD),
            first_send.at[c], first_recv.at[c], device_id=via, device_id_type=MESH)

    def leg_2(c):
        return pltpu.make_async_remote_copy(
            unit(relay_buf, c - FORWARD), unit(far_buf, c),
            middle_send.at[c - FORWARD], middle_recv.at[c - FORWARD],
            device_id=relayed_to, device_id_type=MESH)

    def leg_3(c):
        return pltpu.make_async_remote_copy(
            unit(far_buf, c), unit(near_buf, c),
            last_send.at[c], last_recv.at[c], device_id=ahead, device_id_type=MESH)

    tail = pl.ds(COLS - LANES, LANES)
    edge_s = pltpu.make_async_remote_copy(
        shift_ref.at[:, tail], shift_tile.at[0], edge_send.at[0], edge_recv.at[0],
        device_id=after, device_id_type=MESH)
    edge_f = pltpu.make_async_remote_copy(
        frac_ref.at[:, tail], frac_tile.at[0], edge_send.at[1], edge_recv.at[1],
        device_id=after, device_id_type=MESH)
    edge_s.start()
    edge_f.start()
    direct(0).start()
    leg_1(FORWARD).start()
    direct(1).start()
    leg_1(FORWARD + 1).start()

    lane = lax.broadcasted_iota(jnp.int32, (TR, LANES), 1)
    zero = jnp.zeros((CR, TR, LANES), jnp.float32)
    work[0] = zero
    work[1] = zero
    work[WIDTH - 1] = zero
    cell = lax.broadcasted_iota(jnp.int32, (COLS, LANES), 0)
    face = lax.broadcasted_iota(jnp.int32, (COLS, LANES), 1)
    ones_mat[0:COLS, :] = jnp.where(cell < face * BLOCK, 1.0, 0.0)
    ones_mat[COLS:, :] = jnp.ones((LANES, LANES), jnp.float32)

    for copy in staged:
        copy.wait()
    slot = lax.broadcasted_iota(jnp.int32, (LANES, LANES), 0)
    column = lax.broadcasted_iota(jnp.int32, (LANES, LANES), 1)
    first_hot = jnp.zeros((LANES, LANES), jnp.float32)
    second_hot = first_hot
    code = first_hot
    for j in range(16):
        owner = owner_ref[0, j]
        earlier = jnp.int32(0)
        for i in range(j):
            earlier = earlier + jnp.where(owner_ref[0, i] == owner, 1, 0)
        at = owner * 8 + 2 * earlier
        here = column == source_ref[0, j] + 1
        label = (parity_ref[0, j] * 32 + place_ref[0, j] + 1).astype(jnp.float32)
        first_hot = jnp.where((slot == at) & here, 1.0, first_hot)
        second_hot = jnp.where((slot == at + 1) & here, 1.0, second_hot)
        code = jnp.where((slot == at + 4) | (slot == at + 5), label, code)
    hot_a[...] = first_hot
    hot_b[...] = second_hot
    codes[...] = code

    edge_s.wait_recv()
    edge_f.wait_recv()
    least = jnp.min(jnp.min(shift_tile[...], axis=0), axis=1, keepdims=True)
    least_v[...] = jnp.broadcast_to(least, (ROWS, LANES))
    least_copy = pltpu.make_async_copy(least_v, least_s, least_sem)
    least_copy.start()

    def one_row(local, c):
        r = c * CR + local
        low = least_s[r, 0]
        start = OWN * LANES - LANES - 5 - low
        tile = start // LANES
        turn = start % LANES
        piece = []
        for j in range(11):
            piece.append(pltpu.roll(work[tile + j, local], (LANES - turn) % LANES, 1))
        moved = [jnp.where(lane < LANES - turn, piece[j], piece[j + 1]) for j in range(10)]
        cells = [shifted(moved, 5 - i) for i in range(6)]
        gains = []
        for j in range(9):
            n = shift_tile[j, pl.ds(r, TR, stride=0), :]
            f = frac_tile[j, pl.ds(r, TR, stride=0), :]
            offset = n - low
            upwind = cells[0][j]
            before = cells[1][j]
            passed = jnp.zeros((TR, LANES), jnp.float32)
            total = passed
            for step in range(1, 5):
                total = total + cells[step - 1][j]
                hit = offset == step
                upwind = jnp.where(hit, cells[step][j], upwind)
                before = jnp.where(hit, cells[step + 1][j], before)
                passed = jnp.where(hit, total, passed)
            gains.append(passed + f * upwind + (upwind - before) * (f * (1.0 - f) * 0.5))
        back = [pltpu.roll(gain, 1, 1) for gain in gains]
        at_lhs = pl.ds(pl.multiple_of(local * TR, TR), TR)
        for j in range(1, 9):
            advected = cells[0][j] + jnp.where(lane == 0, back[j - 1], back[j]) - gains[j]
            out_ref[r, :, (j - 1) * LANES : j * LANES] = advected
            own = work[OWN + j - 1, local]
            lhs[at_lhs, pl.ds((j - 1) * LANES, LANES)] = own - advected
        whole = jnp.where(lane == LANES - 1, gains[0], 0.0)
        for j in range(PAD, OWN):
            reached = lane >= (OWN - j) * LANES - low
            whole = whole + jnp.where(reached, work[j, local], 0.0)
        lhs[at_lhs, pl.ds(COLS, LANES)] = whole
        return c

    def finish(c):
        forward(c).wait_recv()
        for j in range(TILES):
            work[PAD + j] = jnp.where(s >= 2, jnp.transpose(far_buf[:, c, j], (1, 0, 2)), 0.0)
            work[PAD + TILES + j] = jnp.where(
                s >= 1, jnp.transpose(near_buf[:, c, j], (1, 0, 2)), 0.0)
            work[OWN + j] = jnp.transpose(own_buf[:, c, j], (1, 0, 2))
        lax.fori_loop(0, CR, one_row, c, unroll=4)
        faces[pl.ds(pl.multiple_of(c * CR * TR, CR * TR), CR * TR), :] = jnp.dot(
            lhs[...], ones_mat[...], precision=HIGHEST, preferred_element_type=jnp.float32)

    def pass_on(c):
        direct(c).wait_recv()
        forward(c).start()

    def first_on(c):
        leg_1(c).wait_recv()
        leg_2(c).start()

    def second_on(c):
        leg_2(c).wait_recv()
        leg_3(c).start()

    def next_direct(c):
        direct(c).wait_send()
        direct(c + 2).start()

    pass_on(0)
    next_direct(0)
    first_on(5)
    leg_1(5).wait_send()
    leg_1(7).start()
    pass_on(1)
    next_direct(1)
    first_on(6)
    second_on(5)
    own_copy.wait()
    least_copy.wait()
    pass_on(2)
    next_direct(2)
    first_on(7)
    second_on(6)
    finish(0)
    pass_on(3)
    second_on(7)
    finish(1)
    finish(5)
    pass_on(4)
    finish(2)
    finish(6)
    finish(3)
    finish(7)
    finish(4)

    pairs = faces[...].reshape(ROWS // 2, 2, TR, LANES)
    fine = (0.5 * (pairs[:, 0] + pairs[:, 1])).reshape(ROWS // 2 * TR, LANES)
    across = (((1,), (1,)), ((), ()))
    half = ROWS // 4 * TR
    packed = (
        lax.dot_general(hot_a[...], fine[:half], across, precision=HIGHEST,
                        preferred_element_type=jnp.float32)
        + lax.dot_general(hot_b[...], fine[half:], across, precision=HIGHEST,
                          preferred_element_type=jnp.float32)
        + codes[...]
    )
    send_buf[...] = packed.reshape(16, 8, LANES)

    def message(other, other_row, slot_base, k):
        return pltpu.make_async_remote_copy(
            send_buf.at[other], recv_buf.at[slot_base + s], msg_send.at[k], msg_recv,
            device_id=(other, other_row), device_id_type=MESH)

    to_self = pltpu.make_async_copy(send_buf.at[s], recv_buf.at[s], msg_recv)
    to_self.start()
    message(s, partner, 16, 0).start()

    def send_out(step, carry):
        other = (s + step) % 16
        message(other, row, 0, 2 * step).start()
        message(other, partner, 16, 2 * step + 1).start()
        return carry

    lax.fori_loop(1, 16, send_out, 0)

    for c in range(CHUNKS):
        forward(c).wait_send()
    for c in (3, 4):
        direct(c).wait_send()
    for c in (5, 6, 7):
        if c != 5:
            leg_1(c).wait_send()
        leg_2(c).wait_send()
    edge_s.wait_send()
    edge_f.wait_send()

    pltpu.make_async_copy(recv_buf, recv_buf, msg_recv).wait()

    received = recv_buf[...]
    names = pltpu.roll(received, 4, 1).reshape(2 * LANES, LANES)
    received = received.reshape(2 * LANES, LANES)
    part = lax.broadcasted_iota(jnp.int32, (2 * LANES, LANES), 0) % 8
    spot = lax.broadcasted_iota(jnp.int32, (2 * LANES, LANES), 1)
    down = (((0,), (0,)), ((), ()))
    sums = []
    counts = []
    for side in range(2):
        wanted = jnp.where(spot < 16, (row % 2) * 32 + 2 * spot + side + 1, -1).astype(jnp.float32)
        found = names == wanted
        for h in range(2):
            hot = jnp.where(found & ((part == h) | (part == h + 2)), 1.0, 0.0)
            sums.append(lax.dot_general(received, hot, down, precision=HIGHEST,
                                        preferred_element_type=jnp.float32))
            if h == 0:
                counts.append(jnp.dot(jnp.ones((8, 2 * LANES), jnp.float32), hot,
                                      preferred_element_type=jnp.float32))
    for side in range(2):
        for h in range(2):
            lhs[0:LANES // 2, (side * 4 + h * 2) * LANES:(side * 4 + h * 2 + 1) * LANES] = (
                sums[side * 2 + h][:LANES // 2])
            lhs[0:LANES // 2, (side * 4 + h * 2 + 1) * LANES:(side * 4 + h * 2 + 2) * LANES] = (
                sums[side * 2 + h][LANES // 2:])

    for side in range(2):
        for quarter in range(4):
            def fix(k, carry):
                r = side * 32 + quarter * 8 + k
                total = lhs[pl.ds(pl.multiple_of(k * TR, TR), TR),
                            pl.ds((side * 4 + quarter) * LANES, LANES)]
                left = faces[pl.ds(pl.multiple_of(r * TR, TR), TR), :]
                change = 0.5 * (total - counts[side] * left)
                for j in range(8):
                    at_start = change if j == 0 else pltpu.roll(change, LANES - 2 * j, 1)
                    at_middle = pltpu.roll(change, 63 - 2 * j, 1)
                    add = jnp.where(lane == 0, at_start, jnp.where(lane == 64, at_middle, 0.0))
                    out_ref[r, :, j * LANES : (j + 1) * LANES] += add
                return carry

            lax.fori_loop(0, 8, fix, 0)

    message(s, partner, 16, 0).wait_send()

    def clean_message(step, carry):
        other = (s + step) % 16
        message(other, row, 0, 2 * step).wait_send()
        message(other, partner, 16, 2 * step + 1).wait_send()
        return carry

    lax.fori_loop(1, 16, clean_message, 0)


def per_device(
    tracers, shifts, fractions, record_owner, record_source, record_parity, record_place
):
    tiled = (TR, CHUNKS, TILES, CR, LANES)
    in_tiles = jnp.transpose(tracers.reshape(TR, CHUNKS, CR, TILES, LANES), (0, 1, 3, 2, 4))
    hbm = pl.BlockSpec(memory_space=pltpu.HBM)
    f32 = jnp.float32
    dma = pltpu.SemaphoreType.DMA
    swept = pl.pallas_call(
        sweep_kernel,
        out_shape=jax.ShapeDtypeStruct((ROWS, TR, COLS), f32),
        in_specs=[hbm] * 7,
        out_specs=pl.BlockSpec(memory_space=pltpu.VMEM),
        scratch_shapes=[
            pltpu.SMEM((1, 16), jnp.int32),
            pltpu.SMEM((1, 16), jnp.int32),
            pltpu.SMEM((1, 16), jnp.int32),
            pltpu.SMEM((1, 16), jnp.int32),
            pltpu.VMEM(tiled, f32),
            pltpu.VMEM(tiled, f32),
            pltpu.VMEM(tiled, f32),
            pltpu.VMEM((WIDTH, CR, TR, LANES), f32),
            pltpu.VMEM((TR, CHUNKS - FORWARD, TILES, CR, LANES), f32),
            pltpu.VMEM((9, ROWS, LANES), jnp.int32),
            pltpu.VMEM((9, ROWS, LANES), f32),
            pltpu.VMEM((ROWS, LANES), jnp.int32),
            pltpu.SMEM((ROWS, LANES), jnp.int32),
            pltpu.VMEM((CR * TR, COLS + LANES), f32),
            pltpu.VMEM((COLS + LANES, LANES), f32),
            pltpu.VMEM((ROWS * TR, LANES), f32),
            pltpu.VMEM((LANES, LANES), f32),
            pltpu.VMEM((LANES, LANES), f32),
            pltpu.VMEM((LANES, LANES), f32),
            pltpu.VMEM((16, 8, LANES), f32),
            pltpu.VMEM((32, 8, LANES), f32),
            dma, dma((2, TILES)), dma((4,)), dma((2,)), dma((2,)), dma,
            dma((CHUNKS,)), dma((CHUNKS,)),
            dma((CHUNKS - FORWARD,)), dma((CHUNKS - FORWARD,)),
            dma((CHUNKS,)), dma((CHUNKS,)),
            dma((32,)), dma, dma,
        ],
        compiler_params=pltpu.CompilerParams(
            collective_id=0, has_side_effects=True, vmem_limit_bytes=40 << 20),
    )(
        *[pltpu.with_memory_space_constraint(v, pltpu.HBM) for v in (in_tiles, shifts, fractions, record_owner.reshape(1, 16), record_source, record_parity, record_place)]
    )
    return jnp.transpose(swept, (1, 0, 2))


def solution(mesh):
    return jax.shard_map(
        per_device,
        mesh=mesh,
        in_specs=(
            P(None, "rows", "stream"),
            P("rows", "stream"),
            P("rows", "stream"),
            P("rows", "stream", None),
            P("rows", "stream"),
            P("rows", "stream"),
            P("rows", "stream"),
        ),
        out_specs=P(None, "rows", "stream"),
        check_vma=False,
    )
```

```python
import jax
import jax.numpy as jnp
from jax import lax
from jax.experimental import pallas as pl
from jax.experimental.pallas import tpu as pltpu
from jax.sharding import PartitionSpec as P

BLOCK = 64
ROWS = 64
COLS = 1024
TR = 8
LANES = 128
TILES = COLS // LANES
PAD = 2
OWN = PAD + 2 * TILES
WIDTH = OWN + TILES + 1
CHUNKS = 8
CR = ROWS // CHUNKS
FORWARD = 5
MESH = pl.DeviceIdType.MESH


def shifted(pieces, amount):
    if amount == 0:
        return pieces[:-1]
    lane = lax.broadcasted_iota(jnp.int32, (TR, LANES), 1)
    turned = [pltpu.roll(piece, LANES - amount, 1) for piece in pieces]
    return [
        jnp.where(lane < LANES - amount, turned[i], turned[i + 1]) for i in range(len(pieces) - 1)
    ]


def times_hot(value, hot, dims):
    high = value.astype(jnp.bfloat16)
    rest = value - high.astype(jnp.float32)
    middle = rest.astype(jnp.bfloat16)
    last = (rest - middle.astype(jnp.float32)).astype(jnp.bfloat16)
    return sum(
        lax.dot_general(part, hot, dims, preferred_element_type=jnp.float32)
        for part in (last, middle, high)
    )


def sweep_kernel(
    t_ref, shift_ref, frac_ref, owner_in, source_in, parity_in, place_in,
    out_ref,
    owner_ref, source_ref, parity_ref, place_ref, own_buf, near_buf, far_buf, work, relay_buf, shift_tile, frac_tile, least_v, least_s, lhs, ones_mat, faces,
    hots, codes, sums, send_buf, recv_buf,
    own_sem, tile_sem, record_sem, edge_send, edge_recv, least_sem,
    first_send, first_recv, middle_send, middle_recv, last_send, last_recv, msg_send, msg_recv, msg_own,
):
    s = lax.axis_index("stream")
    row = lax.axis_index("rows")
    y, z = s // 4, s % 4
    partner = row + 1 - 2 * (row % 2)
    after = ((s + 1) % 16, row)
    ahead = ((s + 15) % 16, row)
    via = (((y + jnp.where(z == 2, 1, 0)) % 4) * 4 + (z + 3) % 4, row)
    from_z = (z + 1) % 4
    from_s = ((y + jnp.where(from_z == 2, 3, 0)) % 4) * 4 + from_z
    relayed_to = ((from_s + 2) % 16, row)

    barrier = pltpu.get_barrier_semaphore()

    def greet(step, carry):
        other = (s + step) % 16
        pl.semaphore_signal(barrier, inc=1, device_id=(other, row), device_id_type=MESH)
        pl.semaphore_signal(barrier, inc=1, device_id=(other, partner), device_id_type=MESH)
        return carry

    lax.fori_loop(1, 16, greet, 0)
    pl.semaphore_signal(barrier, inc=1, device_id=(s, partner), device_id_type=MESH)
    own_copy = pltpu.make_async_copy(t_ref, own_buf, own_sem)
    own_copy.start()
    staged = [
        pltpu.make_async_copy(source, target, record_sem.at[i])
        for i, (source, target) in enumerate(
            [(owner_in, owner_ref), (source_in, source_ref), (parity_in, parity_ref), (place_in, place_ref)])
    ] + [
        pltpu.make_async_copy(source.at[:, pl.ds(j * LANES, LANES)], target.at[j + 1], tile_sem.at[i, j])
        for i, (source, target) in enumerate([(shift_ref, shift_tile), (frac_ref, frac_tile)])
        for j in range(TILES)
    ]
    for copy in staged:
        copy.start()
    pl.semaphore_wait(barrier, 31)

    def unit(ref, c):
        return ref.at[:, c]

    def direct(c):
        return pltpu.make_async_remote_copy(
            unit(t_ref, c), unit(near_buf, c),
            first_send.at[c], first_recv.at[c], device_id=after, device_id_type=MESH)

    def forward(c):
        return pltpu.make_async_remote_copy(
            unit(near_buf, c), unit(far_buf, c),
            last_send.at[c], last_recv.at[c], device_id=after, device_id_type=MESH)

    def leg_1(c):
        return pltpu.make_async_remote_copy(
            unit(t_ref, c), unit(relay_buf, c - FORWARD),
            first_send.at[c], first_recv.at[c], device_id=via, device_id_type=MESH)

    def leg_2(c):
        return pltpu.make_async_remote_copy(
            unit(relay_buf, c - FORWARD), unit(far_buf, c),
            middle_send.at[c - FORWARD], middle_recv.at[c - FORWARD],
            device_id=relayed_to, device_id_type=MESH)

    def leg_3(c):
        return pltpu.make_async_remote_copy(
            unit(far_buf, c), unit(near_buf, c),
            last_send.at[c], last_recv.at[c], device_id=ahead, device_id_type=MESH)

    tail = pl.ds(COLS - LANES, LANES)
    edge_s = pltpu.make_async_remote_copy(
        shift_ref.at[:, tail], shift_tile.at[0], edge_send.at[0], edge_recv.at[0],
        device_id=after, device_id_type=MESH)
    edge_f = pltpu.make_async_remote_copy(
        frac_ref.at[:, tail], frac_tile.at[0], edge_send.at[1], edge_recv.at[1],
        device_id=after, device_id_type=MESH)
    edge_s.start()
    edge_f.start()
    direct(0).start()
    leg_1(FORWARD).start()
    direct(1).start()
    leg_1(FORWARD + 1).start()

    lane = lax.broadcasted_iota(jnp.int32, (TR, LANES), 1)
    zero = jnp.zeros((CR, TR, LANES), jnp.float32)
    work[0] = zero
    work[1] = zero
    work[WIDTH - 1] = zero
    cell = lax.broadcasted_iota(jnp.int32, (COLS, LANES), 0)
    face_lane = lax.broadcasted_iota(jnp.int32, (COLS, LANES), 1)
    face = 2 * (face_lane % 64) + face_lane // 64
    ones_mat[0:COLS, :] = jnp.where(cell < face * BLOCK, 1.0, 0.0).astype(jnp.bfloat16)
    ones_mat[COLS:, :] = jnp.ones((LANES, LANES), jnp.bfloat16)

    for copy in staged:
        copy.wait()
    slot = lax.broadcasted_iota(jnp.int32, (LANES, LANES), 0)
    column = lax.broadcasted_iota(jnp.int32, (LANES, LANES), 1)
    first_hot = jnp.zeros((LANES, LANES), jnp.float32)
    second_hot = first_hot
    code = first_hot
    for j in range(16):
        owner = owner_ref[0, j]
        earlier = jnp.int32(0)
        for i in range(j):
            earlier = earlier + jnp.where(owner_ref[0, i] == owner, 1, 0)
        at = owner * 8 + 2 * earlier
        at_face = source_ref[0, j] + 1
        here = column == (at_face % 2) * 64 + at_face // 2
        label = (parity_ref[0, j] * 32 + place_ref[0, j] + 1).astype(jnp.float32)
        first_hot = jnp.where((slot == at) & here, 1.0, first_hot)
        second_hot = jnp.where((slot == at + 1) & here, 1.0, second_hot)
        code = jnp.where((slot == at + 4) | (slot == at + 5), label, code)
    hots[0] = first_hot.astype(jnp.bfloat16)
    hots[1] = second_hot.astype(jnp.bfloat16)
    codes[...] = code

    edge_s.wait_recv()
    edge_f.wait_recv()
    least = jnp.min(jnp.min(shift_tile[...], axis=0), axis=1, keepdims=True)
    least_v[...] = jnp.broadcast_to(least, (ROWS, LANES))
    least_copy = pltpu.make_async_copy(least_v, least_s, least_sem)
    least_copy.start()

    def one_row(local, c):
        r = c * CR + local
        low = least_s[r, 0]
        start = OWN * LANES - LANES - 5 - low
        tile = start // LANES
        turn = start % LANES
        piece = []
        for j in range(11):
            piece.append(pltpu.roll(work[tile + j, local], (LANES - turn) % LANES, 1))
        moved = [jnp.where(lane < LANES - turn, piece[j], piece[j + 1]) for j in range(10)]
        cells = [shifted(moved, 5 - i) for i in range(6)]
        gains = []
        for j in range(9):
            n = shift_tile[j, pl.ds(r, TR, stride=0), :]
            f = frac_tile[j, pl.ds(r, TR, stride=0), :]
            offset = n - low
            upwind = cells[0][j]
            before = cells[1][j]
            passed = jnp.zeros((TR, LANES), jnp.float32)
            total = passed
            for step in range(1, 5):
                total = total + cells[step - 1][j]
                hit = offset == step
                upwind = jnp.where(hit, cells[step][j], upwind)
                before = jnp.where(hit, cells[step + 1][j], before)
                passed = jnp.where(hit, total, passed)
            gains.append(passed + f * upwind + (upwind - before) * (f * (1.0 - f) * 0.5))
        back = [pltpu.roll(gain, 1, 1) for gain in gains]
        at_lhs = pl.ds(pl.multiple_of(local * TR, TR), TR)
        for j in range(1, 9):
            advected = cells[0][j] + jnp.where(lane == 0, back[j - 1], back[j]) - gains[j]
            out_ref[r, :, (j - 1) * LANES : j * LANES] = advected
            own = work[OWN + j - 1, local]
            lhs[at_lhs, pl.ds((j - 1) * LANES, LANES)] = own - advected
        whole = jnp.where(lane == LANES - 1, gains[0], 0.0)
        for j in range(PAD, OWN):
            reached = lane >= (OWN - j) * LANES - low
            whole = whole + jnp.where(reached, work[j, local], 0.0)
        lhs[at_lhs, pl.ds(COLS, LANES)] = whole
        return c

    def finish(c):
        forward(c).wait_recv()
        for j in range(TILES):
            work[PAD + j] = jnp.where(s >= 2, jnp.transpose(far_buf[:, c, j], (1, 0, 2)), 0.0)
            work[PAD + TILES + j] = jnp.where(
                s >= 1, jnp.transpose(near_buf[:, c, j], (1, 0, 2)), 0.0)
            work[OWN + j] = jnp.transpose(own_buf[:, c, j], (1, 0, 2))
        lax.fori_loop(0, CR, one_row, c, unroll=8)
        faces[pl.ds(pl.multiple_of(c * CR * TR, CR * TR), CR * TR), :] = times_hot(
            lhs[...], ones_mat[...], (((1,), (0,)), ((), ())))

    across = (((1,), (1,)), ((), ()))
    half = ROWS // 4 * TR

    def pack(h):
        pairs = faces[2 * h * half : 2 * (h + 1) * half, :].reshape(ROWS // 4, 2, TR, LANES)
        fine = (0.5 * (pairs[:, 0] + pairs[:, 1])).reshape(half, LANES)
        high = fine.astype(jnp.bfloat16)
        rest = fine - high.astype(jnp.float32)
        middle = rest.astype(jnp.bfloat16)
        last = (rest - middle.astype(jnp.float32)).astype(jnp.bfloat16)
        hot = hots[h]
        return sum(
            lax.dot_general(hot, part, across, preferred_element_type=jnp.float32)
            for part in (last, middle, high))

    def pass_on(c):
        direct(c).wait_recv()
        forward(c).start()

    def first_on(c):
        leg_1(c).wait_recv()
        leg_2(c).start()

    def second_on(c):
        leg_2(c).wait_recv()
        leg_3(c).start()

    def next_direct(c):
        direct(c).wait_send()
        direct(c + 2).start()

    pass_on(0)
    next_direct(0)
    first_on(5)
    leg_1(5).wait_send()
    leg_1(7).start()
    pass_on(1)
    next_direct(1)
    first_on(6)
    second_on(5)
    own_copy.wait()
    least_copy.wait()
    pass_on(2)
    next_direct(2)
    first_on(7)
    second_on(6)
    finish(0)
    pass_on(3)
    second_on(7)
    finish(1)
    finish(5)
    pass_on(4)
    finish(2)
    finish(6)
    finish(3)
    codes[...] += pack(0)
    finish(7)
    finish(4)

    packed = codes[...] + pack(1)
    send_buf[...] = packed.reshape(16, 8, LANES)

    def message(other, other_row, slot_base, k):
        return pltpu.make_async_remote_copy(
            send_buf.at[other], recv_buf.at[slot_base + s], msg_send.at[k], msg_recv,
            device_id=(other, other_row), device_id_type=MESH)

    to_self = pltpu.make_async_copy(send_buf.at[s], recv_buf.at[s], msg_recv)
    to_self.start()
    message(s, partner, 16, 0).start()

    def send_out(step, carry):
        other = (s + step) % 16
        message(other, row, 0, 2 * step).start()
        message(other, partner, 16, 2 * step + 1).start()
        return carry

    lax.fori_loop(1, 16, send_out, 0)

    for c in range(CHUNKS):
        forward(c).wait_send()
    for c in (3, 4):
        direct(c).wait_send()
    for c in (5, 6, 7):
        if c != 5:
            leg_1(c).wait_send()
        leg_2(c).wait_send()
    edge_s.wait_send()
    edge_f.wait_send()

    pltpu.make_async_copy(recv_buf, recv_buf, msg_recv).wait()

    received = recv_buf[...]
    names = pltpu.roll(received, 4, 1).reshape(2 * LANES, LANES)
    received = received.reshape(2 * LANES, LANES)
    part = lax.broadcasted_iota(jnp.int32, (2 * LANES, LANES), 0) % 8
    spot = lax.broadcasted_iota(jnp.int32, (2 * LANES, LANES), 1)
    group = spot % 64 // TILES
    block = 2 * (spot % TILES) + spot // 64
    wanted = jnp.where(group < 4, (row % 2) * 32 + 2 * block + group % 2 + 1, -1).astype(jnp.float32)
    hot = jnp.where((names == wanted) & ((part == group // 2) | (part == group // 2 + 2)), 1.0, 0.0)
    hot = hot.astype(jnp.bfloat16)
    down = (((0,), (0,)), ((), ()))
    sums[...] = times_hot(received, hot, down)
    count = jnp.dot(jnp.ones((TR, 2 * LANES), jnp.bfloat16), hot, preferred_element_type=jnp.float32)

    for side in range(2):
        count_here = count if side == 0 else pltpu.roll(count, LANES - side * TILES, 1)
        for h in range(2):
            base = side * 32 + h * 16
            back = (LANES - (h * 2 + side) * TILES) % LANES

            def fix(k, carry, base=base, back=back, count_here=count_here):
                r = base + k
                sent = sums[pl.ds(pl.multiple_of(k * TR, TR), TR), :]
                sent = pltpu.roll(sent, back, 1) if back else sent
                left = faces[pl.ds(pl.multiple_of(r * TR, TR), TR), :]
                change = 0.5 * (sent - count_here * left)
                for j in range(TILES):
                    turned = pltpu.roll(change, LANES - j, 1) if j else change
                    out_ref[r, :, j * LANES : (j + 1) * LANES] += jnp.where(
                        lane % 64 == 0, turned, 0.0)
                return carry

            lax.fori_loop(0, 16, fix, 0, unroll=4)

    message(s, partner, 16, 0).wait_send()

    def clean_message(step, carry):
        other = (s + step) % 16
        message(other, row, 0, 2 * step).wait_send()
        message(other, partner, 16, 2 * step + 1).wait_send()
        return carry

    lax.fori_loop(1, 16, clean_message, 0)


def per_device(
    tracers, shifts, fractions, record_owner, record_source, record_parity, record_place
):
    tiled = (TR, CHUNKS, TILES, CR, LANES)
    in_tiles = jnp.transpose(tracers.reshape(TR, CHUNKS, CR, TILES, LANES), (0, 1, 3, 2, 4))
    hbm = pl.BlockSpec(memory_space=pltpu.HBM)
    f32 = jnp.float32
    dma = pltpu.SemaphoreType.DMA
    swept = pl.pallas_call(
        sweep_kernel,
        out_shape=jax.ShapeDtypeStruct((ROWS, TR, COLS), f32),
        in_specs=[hbm] * 7,
        out_specs=pl.BlockSpec(memory_space=pltpu.VMEM),
        scratch_shapes=[
            pltpu.SMEM((1, 16), jnp.int32),
            pltpu.SMEM((1, 16), jnp.int32),
            pltpu.SMEM((1, 16), jnp.int32),
            pltpu.SMEM((1, 16), jnp.int32),
            pltpu.VMEM(tiled, f32),
            pltpu.VMEM(tiled, f32),
            pltpu.VMEM(tiled, f32),
            pltpu.VMEM((WIDTH, CR, TR, LANES), f32),
            pltpu.VMEM((TR, CHUNKS - FORWARD, TILES, CR, LANES), f32),
            pltpu.VMEM((9, ROWS, LANES), jnp.int32),
            pltpu.VMEM((9, ROWS, LANES), f32),
            pltpu.VMEM((ROWS, LANES), jnp.int32),
            pltpu.SMEM((ROWS, LANES), jnp.int32),
            pltpu.VMEM((CR * TR, COLS + LANES), f32),
            pltpu.VMEM((COLS + LANES, LANES), jnp.bfloat16),
            pltpu.VMEM((ROWS * TR, LANES), f32),
            pltpu.VMEM((2, LANES, LANES), jnp.bfloat16),
            pltpu.VMEM((LANES, LANES), f32),
            pltpu.VMEM((LANES, LANES), f32),
            pltpu.VMEM((16, 8, LANES), f32),
            pltpu.VMEM((32, 8, LANES), f32),
            dma, dma((2, TILES)), dma((4,)), dma((2,)), dma((2,)), dma,
            dma((CHUNKS,)), dma((CHUNKS,)),
            dma((CHUNKS - FORWARD,)), dma((CHUNKS - FORWARD,)),
            dma((CHUNKS,)), dma((CHUNKS,)),
            dma((32,)), dma, dma,
        ],
        compiler_params=pltpu.CompilerParams(
            collective_id=0, has_side_effects=True, vmem_limit_bytes=40 << 20),
    )(
        *[pltpu.with_memory_space_constraint(v, pltpu.HBM) for v in (in_tiles, shifts, fractions, record_owner.reshape(1, 16), record_source, record_parity, record_place)]
    )
    return jnp.transpose(swept, (1, 0, 2))


def solution(mesh):
    return jax.shard_map(
        per_device,
        mesh=mesh,
        in_specs=(
            P(None, "rows", "stream"),
            P("rows", "stream"),
            P("rows", "stream"),
            P("rows", "stream", None),
            P("rows", "stream"),
            P("rows", "stream"),
            P("rows", "stream"),
        ),
        out_specs=P(None, "rows", "stream"),
        check_vma=False,
    )
```

```python
import jax
import jax.numpy as jnp
from jax import lax
from jax.experimental import pallas as pl
from jax.experimental.pallas import tpu as pltpu
from jax.sharding import PartitionSpec as P

BLOCK = 64
ROWS = 64
COLS = 1024
TR = 8
LANES = 128
TILES = COLS // LANES
PAD = 2
OWN = PAD + 2 * TILES
WIDTH = OWN + TILES + 1
CHUNKS = 8
CR = ROWS // CHUNKS
PIECES = ((0, 0, 8), (1, 0, 8), (2, 0, 8), (3, 0, 8), (4, 0, 8), (5, 0, 8), (6, 0, 8), (7, 0, 8))
PLUS = 5
AHEAD = 4
AHEAD_MINUS = 3
FAR_FIRST = (10, 9, 11, 6, 14, 2, 8, 5, 7, 13, 15, 1, 3, 4, 12)
MINUS = len(PIECES) - PLUS
MESH = pl.DeviceIdType.MESH


def shifted(pieces, amount):
    if amount == 0:
        return pieces[:-1]
    lane = lax.broadcasted_iota(jnp.int32, (TR, LANES), 1)
    turned = [pltpu.roll(piece, LANES - amount, 1) for piece in pieces]
    return [
        jnp.where(lane < LANES - amount, turned[i], turned[i + 1]) for i in range(len(pieces) - 1)
    ]


def times_hot(value, hot, dims):
    high = value.astype(jnp.bfloat16)
    rest = value - high.astype(jnp.float32)
    middle = rest.astype(jnp.bfloat16)
    last = (rest - middle.astype(jnp.float32)).astype(jnp.bfloat16)
    return sum(
        lax.dot_general(part, hot, dims, preferred_element_type=jnp.float32)
        for part in (last, middle, high)
    )


def sweep_kernel(
    t_ref, shift_ref, frac_ref, owner_in, source_in, parity_in, place_in,
    out_ref,
    owner_ref, source_ref, parity_ref, place_ref, own_buf, near_buf, far_buf, work, relay_buf, shift_tile, frac_tile, least_v, least_s, lhs, ones_mat, faces,
    hots, codes, sums, send_buf, recv_buf,
    own_sem, tile_sem, record_sem, edge_send, edge_recv, least_sem,
    first_send, first_recv, middle_send, middle_recv, last_send, last_recv, msg_send, msg_recv, msg_own,
):
    s = lax.axis_index("stream")
    row = lax.axis_index("rows")
    y, z = s // 4, s % 4
    partner = row + 1 - 2 * (row % 2)
    after = ((s + 1) % 16, row)
    ahead = ((s + 15) % 16, row)
    via = (((y + jnp.where(z == 2, 1, 0)) % 4) * 4 + (z + 3) % 4, row)
    from_z = (z + 1) % 4
    from_s = ((y + jnp.where(from_z == 2, 3, 0)) % 4) * 4 + from_z
    relayed_to = ((from_s + 2) % 16, row)

    barrier = pltpu.get_barrier_semaphore()

    def greet(step, carry):
        other = (s + step) % 16
        pl.semaphore_signal(barrier, inc=1, device_id=(other, row), device_id_type=MESH)
        pl.semaphore_signal(barrier, inc=1, device_id=(other, partner), device_id_type=MESH)
        return carry

    lax.fori_loop(1, 16, greet, 0)
    pl.semaphore_signal(barrier, inc=1, device_id=(s, partner), device_id_type=MESH)
    own_copy = pltpu.make_async_copy(t_ref, own_buf, own_sem)
    own_copy.start()
    staged = [
        pltpu.make_async_copy(source, target, record_sem.at[i])
        for i, (source, target) in enumerate(
            [(owner_in, owner_ref), (source_in, source_ref), (parity_in, parity_ref), (place_in, place_ref)])
    ] + [
        pltpu.make_async_copy(source.at[:, pl.ds(j * LANES, LANES)], target.at[j + 1], tile_sem.at[i, j])
        for i, (source, target) in enumerate([(shift_ref, shift_tile), (frac_ref, frac_tile)])
        for j in range(TILES)
    ]
    for copy in staged:
        copy.start()
    pl.semaphore_wait(barrier, 31)

    def unit(ref, p):
        block, first, many = PIECES[p]
        return ref.at[pl.ds(first, many), block]

    def parked(p):
        _, first, many = PIECES[p]
        return relay_buf.at[pl.ds(first, many), p - PLUS]

    def send(source, target, send_sem, recv_sem, device):
        return pltpu.make_async_remote_copy(
            source, target, send_sem, recv_sem, device_id=device, device_id_type=MESH)

    def direct(p):
        return send(unit(t_ref, p), unit(near_buf, p), first_send.at[p], first_recv.at[p], after)

    def forward(p):
        return send(unit(near_buf, p), unit(far_buf, p), last_send.at[p], last_recv.at[p], after)

    def leg_1(p):
        return send(unit(t_ref, p), parked(p), first_send.at[p], first_recv.at[p], via)

    def leg_2(p):
        return send(parked(p), unit(far_buf, p), middle_send.at[p - PLUS],
                    middle_recv.at[p - PLUS], relayed_to)

    def leg_3(p):
        return send(unit(far_buf, p), unit(near_buf, p), last_send.at[p], last_recv.at[p], ahead)

    tail = pl.ds(COLS - LANES, LANES)
    edge_s = pltpu.make_async_remote_copy(
        shift_ref.at[:, tail], shift_tile.at[0], edge_send.at[0], edge_recv.at[0],
        device_id=after, device_id_type=MESH)
    edge_f = pltpu.make_async_remote_copy(
        frac_ref.at[:, tail], frac_tile.at[0], edge_send.at[1], edge_recv.at[1],
        device_id=after, device_id_type=MESH)
    edge_s.start()
    edge_f.start()
    for i in range(max(AHEAD, AHEAD_MINUS)):
        if i < AHEAD:
            direct(i).start()
        if i < AHEAD_MINUS:
            leg_1(PLUS + i).start()

    lane = lax.broadcasted_iota(jnp.int32, (TR, LANES), 1)
    zero = jnp.zeros((CR, TR, LANES), jnp.float32)
    work[0] = zero
    work[1] = zero
    work[WIDTH - 1] = zero
    cell = lax.broadcasted_iota(jnp.int32, (COLS, LANES), 0)
    face_lane = lax.broadcasted_iota(jnp.int32, (COLS, LANES), 1)
    face = 2 * (face_lane % 64) + face_lane // 64
    ones_mat[0:COLS, :] = jnp.where(cell < face * BLOCK, 1.0, 0.0).astype(jnp.bfloat16)
    ones_mat[COLS:, :] = jnp.ones((LANES, LANES), jnp.bfloat16)

    for copy in staged:
        copy.wait()
    slot = lax.broadcasted_iota(jnp.int32, (LANES, LANES), 0)
    column = lax.broadcasted_iota(jnp.int32, (LANES, LANES), 1)
    first_hot = jnp.zeros((LANES, LANES), jnp.float32)
    second_hot = first_hot
    code = first_hot
    for j in range(16):
        owner = owner_ref[0, j]
        earlier = jnp.int32(0)
        for i in range(j):
            earlier = earlier + jnp.where(owner_ref[0, i] == owner, 1, 0)
        at = owner * 8 + 2 * earlier
        at_face = source_ref[0, j] + 1
        here = column == (at_face % 2) * 64 + at_face // 2
        label = (parity_ref[0, j] * 32 + place_ref[0, j] + 1).astype(jnp.float32)
        first_hot = jnp.where((slot == at) & here, 1.0, first_hot)
        second_hot = jnp.where((slot == at + 1) & here, 1.0, second_hot)
        code = jnp.where((slot == at + 4) | (slot == at + 5), label, code)
    hots[0] = first_hot.astype(jnp.bfloat16)
    hots[1] = second_hot.astype(jnp.bfloat16)
    codes[...] = code

    edge_s.wait_recv()
    edge_f.wait_recv()
    least = jnp.min(jnp.min(shift_tile[...], axis=0), axis=1, keepdims=True)
    least_v[...] = jnp.broadcast_to(least, (ROWS, LANES))
    least_copy = pltpu.make_async_copy(least_v, least_s, least_sem)
    least_copy.start()

    def one_row(local, c):
        r = c * CR + local
        low = least_s[r, 0]
        start = OWN * LANES - LANES - 5 - low
        tile = start // LANES
        turn = start % LANES
        piece = []
        for j in range(11):
            piece.append(pltpu.roll(work[tile + j, local], (LANES - turn) % LANES, 1))
        moved = [jnp.where(lane < LANES - turn, piece[j], piece[j + 1]) for j in range(10)]
        cells = [shifted(moved, 5 - i) for i in range(6)]
        gains = []
        for j in range(9):
            n = shift_tile[j, pl.ds(r, TR, stride=0), :]
            f = frac_tile[j, pl.ds(r, TR, stride=0), :]
            offset = n - low
            upwind = cells[0][j]
            before = cells[1][j]
            passed = jnp.zeros((TR, LANES), jnp.float32)
            total = passed
            for step in range(1, 5):
                total = total + cells[step - 1][j]
                hit = offset == step
                upwind = jnp.where(hit, cells[step][j], upwind)
                before = jnp.where(hit, cells[step + 1][j], before)
                passed = jnp.where(hit, total, passed)
            gains.append(passed + f * upwind + (upwind - before) * (f * (1.0 - f) * 0.5))
        back = [pltpu.roll(gain, 1, 1) for gain in gains]
        at_lhs = pl.ds(pl.multiple_of(local * TR, TR), TR)
        for j in range(1, 9):
            advected = cells[0][j] + jnp.where(lane == 0, back[j - 1], back[j]) - gains[j]
            out_ref[r, :, (j - 1) * LANES : j * LANES] = advected
            own = work[OWN + j - 1, local]
            lhs[at_lhs, pl.ds((j - 1) * LANES, LANES)] = own - advected
        whole = jnp.where(lane == LANES - 1, gains[0], 0.0)
        for j in range(PAD, OWN):
            reached = lane >= (OWN - j) * LANES - low
            whole = whole + jnp.where(reached, work[j, local], 0.0)
        lhs[at_lhs, pl.ds(COLS, LANES)] = whole
        return c

    def finish(c):
        for p, piece in enumerate(PIECES):
            if piece[0] == c:
                (forward(p) if p < PLUS else leg_3(p)).wait_recv()
        for j in range(TILES):
            work[PAD + j] = jnp.where(s >= 2, jnp.transpose(far_buf[:, c, j], (1, 0, 2)), 0.0)
            work[PAD + TILES + j] = jnp.where(
                s >= 1, jnp.transpose(near_buf[:, c, j], (1, 0, 2)), 0.0)
            work[OWN + j] = jnp.transpose(own_buf[:, c, j], (1, 0, 2))
        lax.fori_loop(0, CR, one_row, c, unroll=8)
        faces[pl.ds(pl.multiple_of(c * CR * TR, CR * TR), CR * TR), :] = times_hot(
            lhs[...], ones_mat[...], (((1,), (0,)), ((), ())))

    across = (((1,), (1,)), ((), ()))
    half = ROWS // 4 * TR

    def pack(h):
        pairs = faces[2 * h * half : 2 * (h + 1) * half, :].reshape(ROWS // 4, 2, TR, LANES)
        fine = (0.5 * (pairs[:, 0] + pairs[:, 1])).reshape(half, LANES)
        high = fine.astype(jnp.bfloat16)
        rest = fine - high.astype(jnp.float32)
        middle = rest.astype(jnp.bfloat16)
        last = (rest - middle.astype(jnp.float32)).astype(jnp.bfloat16)
        hot = hots[h]
        return sum(
            lax.dot_general(hot, part, across, preferred_element_type=jnp.float32)
            for part in (last, middle, high))

    def pass_on(p):
        direct(p).wait_recv()
        forward(p).start()
        if p + AHEAD < PLUS:
            direct(p).wait_send()
            direct(p + AHEAD).start()

    def first_on(p):
        leg_1(p).wait_recv()
        leg_2(p).start()
        if p + AHEAD_MINUS < len(PIECES):
            leg_1(p).wait_send()
            leg_1(p + AHEAD_MINUS).start()

    def second_on(p):
        leg_2(p).wait_recv()
        leg_3(p).start()

    pass_on(0)
    first_on(5)
    pass_on(1)
    first_on(6)
    pass_on(2)
    first_on(7)
    second_on(5)
    pass_on(3)
    second_on(6)
    pass_on(4)
    second_on(7)
    own_copy.wait()
    least_copy.wait()
    finish(0)
    finish(1)
    finish(2)
    finish(5)
    finish(3)
    codes[...] += pack(0)
    finish(6)
    finish(7)
    finish(4)

    packed = codes[...] + pack(1)
    send_buf[...] = packed.reshape(16, 8, LANES)

    def message(other, other_row, slot_base, k):
        return pltpu.make_async_remote_copy(
            send_buf.at[other], recv_buf.at[slot_base + s], msg_send.at[k], msg_recv,
            device_id=(other, other_row), device_id_type=MESH)

    to_self = pltpu.make_async_copy(send_buf.at[s], recv_buf.at[s], msg_recv)
    to_self.start()
    message(s, partner, 16, 0).start()

    def send_out(step, carry):
        other = (s + step) % 16
        message(other, row, 0, 2 * step).start()
        message(other, partner, 16, 2 * step + 1).start()
        return carry

    for step in FAR_FIRST:
        send_out(step, 0)

    for p in range(len(PIECES)):
        (forward(p) if p < PLUS else leg_3(p)).wait_send()
        if PLUS - AHEAD <= p < PLUS:
            direct(p).wait_send()
        if p >= PLUS:
            leg_2(p).wait_send()
        if p >= len(PIECES) - AHEAD_MINUS:
            leg_1(p).wait_send()
    edge_s.wait_send()
    edge_f.wait_send()

    pltpu.make_async_copy(recv_buf, recv_buf, msg_recv).wait()

    received = recv_buf[...]
    names = pltpu.roll(received, 4, 1).reshape(2 * LANES, LANES)
    received = received.reshape(2 * LANES, LANES)
    part = lax.broadcasted_iota(jnp.int32, (2 * LANES, LANES), 0) % 8
    spot = lax.broadcasted_iota(jnp.int32, (2 * LANES, LANES), 1)
    group = spot % 64 // TILES
    block = 2 * (spot % TILES) + spot // 64
    wanted = jnp.where(group < 4, (row % 2) * 32 + 2 * block + group % 2 + 1, -1).astype(jnp.float32)
    hot = jnp.where((names == wanted) & ((part == group // 2) | (part == group // 2 + 2)), 1.0, 0.0)
    hot = hot.astype(jnp.bfloat16)
    down = (((0,), (0,)), ((), ()))
    sums[...] = times_hot(received, hot, down)
    count = jnp.dot(jnp.ones((TR, 2 * LANES), jnp.bfloat16), hot, preferred_element_type=jnp.float32)

    for side in range(2):
        count_here = count if side == 0 else pltpu.roll(count, LANES - side * TILES, 1)
        for h in range(2):
            base = side * 32 + h * 16
            back = (LANES - (h * 2 + side) * TILES) % LANES

            def fix(k, carry, base=base, back=back, count_here=count_here):
                r = base + k
                sent = sums[pl.ds(pl.multiple_of(k * TR, TR), TR), :]
                sent = pltpu.roll(sent, back, 1) if back else sent
                left = faces[pl.ds(pl.multiple_of(r * TR, TR), TR), :]
                change = 0.5 * (sent - count_here * left)
                for j in range(TILES):
                    turned = pltpu.roll(change, LANES - j, 1) if j else change
                    out_ref[r, :, j * LANES : (j + 1) * LANES] += jnp.where(
                        lane % 64 == 0, turned, 0.0)
                return carry

            lax.fori_loop(0, 16, fix, 0, unroll=16)

    message(s, partner, 16, 0).wait_send()

    def clean_message(step, carry):
        other = (s + step) % 16
        message(other, row, 0, 2 * step).wait_send()
        message(other, partner, 16, 2 * step + 1).wait_send()
        return carry

    lax.fori_loop(1, 16, clean_message, 0)


def per_device(
    tracers, shifts, fractions, record_owner, record_source, record_parity, record_place
):
    tiled = (TR, CHUNKS, TILES, CR, LANES)
    in_tiles = jnp.transpose(tracers.reshape(TR, CHUNKS, CR, TILES, LANES), (0, 1, 3, 2, 4))
    hbm = pl.BlockSpec(memory_space=pltpu.HBM)
    f32 = jnp.float32
    dma = pltpu.SemaphoreType.DMA
    swept = pl.pallas_call(
        sweep_kernel,
        out_shape=jax.ShapeDtypeStruct((ROWS, TR, COLS), f32),
        in_specs=[hbm] * 7,
        out_specs=pl.BlockSpec(memory_space=pltpu.VMEM),
        scratch_shapes=[
            pltpu.SMEM((1, 16), jnp.int32),
            pltpu.SMEM((1, 16), jnp.int32),
            pltpu.SMEM((1, 16), jnp.int32),
            pltpu.SMEM((1, 16), jnp.int32),
            pltpu.VMEM(tiled, f32),
            pltpu.VMEM(tiled, f32),
            pltpu.VMEM(tiled, f32),
            pltpu.VMEM((WIDTH, CR, TR, LANES), f32),
            pltpu.VMEM((TR, MINUS, TILES, CR, LANES), f32),
            pltpu.VMEM((9, ROWS, LANES), jnp.int32),
            pltpu.VMEM((9, ROWS, LANES), f32),
            pltpu.VMEM((ROWS, LANES), jnp.int32),
            pltpu.SMEM((ROWS, LANES), jnp.int32),
            pltpu.VMEM((CR * TR, COLS + LANES), f32),
            pltpu.VMEM((COLS + LANES, LANES), jnp.bfloat16),
            pltpu.VMEM((ROWS * TR, LANES), f32),
            pltpu.VMEM((2, LANES, LANES), jnp.bfloat16),
            pltpu.VMEM((LANES, LANES), f32),
            pltpu.VMEM((LANES, LANES), f32),
            pltpu.VMEM((16, 8, LANES), f32),
            pltpu.VMEM((32, 8, LANES), f32),
            dma, dma((2, TILES)), dma((4,)), dma((2,)), dma((2,)), dma,
            dma((len(PIECES),)), dma((len(PIECES),)), dma((MINUS,)), dma((MINUS,)),
            dma((len(PIECES),)), dma((len(PIECES),)),
            dma((32,)), dma, dma,
        ],
        compiler_params=pltpu.CompilerParams(
            collective_id=0, has_side_effects=True, vmem_limit_bytes=40 << 20),
    )(
        *[pltpu.with_memory_space_constraint(v, pltpu.HBM) for v in (in_tiles, shifts, fractions, record_owner.reshape(1, 16), record_source, record_parity, record_place)]
    )
    return jnp.transpose(swept, (1, 0, 2))


def solution(mesh):
    return jax.shard_map(
        per_device,
        mesh=mesh,
        in_specs=(
            P(None, "rows", "stream"),
            P("rows", "stream"),
            P("rows", "stream"),
            P("rows", "stream", None),
            P("rows", "stream"),
            P("rows", "stream"),
            P("rows", "stream"),
        ),
        out_specs=P(None, "rows", "stream"),
        check_vma=False,
    )
```

```python
import jax
import jax.numpy as jnp
from jax import lax
from jax.experimental import pallas as pl
from jax.experimental.pallas import tpu as pltpu
from jax.sharding import PartitionSpec as P

BLOCK = 64
ROWS = 64
COLS = 1024
TR = 8
LANES = 128
TILES = COLS // LANES
PAD = 2
OWN = PAD + 2 * TILES
WIDTH = OWN + TILES + 1
CHUNKS = 8
CR = ROWS // CHUNKS
PIECES = ((0, 0, 8), (1, 0, 8), (2, 0, 8), (3, 0, 8), (4, 0, 8), (5, 0, 8), (6, 0, 8), (7, 0, 8))
PLUS = 5
AHEAD = 4
AHEAD_MINUS = 3
FAR_FIRST = (10, 9, 11, 6, 14, 2, 8, 5, 7, 13, 15, 1, 3, 4, 12)
MINUS = len(PIECES) - PLUS
MESH = pl.DeviceIdType.MESH


def shifted(pieces, amount):
    if amount == 0:
        return pieces[:-1]
    lane = lax.broadcasted_iota(jnp.int32, (TR, LANES), 1)
    turned = [pltpu.roll(piece, LANES - amount, 1) for piece in pieces]
    return [
        jnp.where(lane < LANES - amount, turned[i], turned[i + 1]) for i in range(len(pieces) - 1)
    ]


def times_hot(value, hot, dims):
    high = value.astype(jnp.bfloat16)
    rest = value - high.astype(jnp.float32)
    middle = rest.astype(jnp.bfloat16)
    last = (rest - middle.astype(jnp.float32)).astype(jnp.bfloat16)
    return sum(
        lax.dot_general(part, hot, dims, preferred_element_type=jnp.float32)
        for part in (last, middle, high)
    )


def sweep_kernel(
    t_ref, shift_ref, frac_ref, owner_in, source_in, parity_in, place_in,
    out_ref,
    owner_ref, source_ref, parity_ref, place_ref, own_buf, near_buf, far_buf, work, relay_buf, shift_tile, frac_tile, least_v, least_s, lhs, ones_mat, faces,
    hots, codes, sums, send_buf, recv_buf,
    own_sem, tile_sem, record_sem, edge_send, edge_recv, least_sem,
    first_send, first_recv, middle_send, middle_recv, last_send, last_recv, msg_send, msg_recv, msg_own,
):
    s = lax.axis_index("stream")
    row = lax.axis_index("rows")
    y, z = s // 4, s % 4
    partner = row + 1 - 2 * (row % 2)
    after = ((s + 1) % 16, row)
    ahead = ((s + 15) % 16, row)
    via = (((y + jnp.where(z == 2, 1, 0)) % 4) * 4 + (z + 3) % 4, row)
    from_z = (z + 1) % 4
    from_s = ((y + jnp.where(from_z == 2, 3, 0)) % 4) * 4 + from_z
    relayed_to = ((from_s + 2) % 16, row)

    barrier = pltpu.get_barrier_semaphore()

    def greet(step, carry):
        other = (s + step) % 16
        pl.semaphore_signal(barrier, inc=1, device_id=(other, row), device_id_type=MESH)
        pl.semaphore_signal(barrier, inc=1, device_id=(other, partner), device_id_type=MESH)
        return carry

    lax.fori_loop(1, 16, greet, 0)
    pl.semaphore_signal(barrier, inc=1, device_id=(s, partner), device_id_type=MESH)
    own_copy = pltpu.make_async_copy(t_ref, own_buf, own_sem)
    own_copy.start()
    staged = [
        pltpu.make_async_copy(source, target, record_sem.at[i])
        for i, (source, target) in enumerate(
            [(owner_in, owner_ref), (source_in, source_ref), (parity_in, parity_ref), (place_in, place_ref)])
    ] + [
        pltpu.make_async_copy(source.at[:, pl.ds(j * LANES, LANES)], target.at[j + 1, pl.ds(0, ROWS)], tile_sem.at[i, j])
        for i, (source, target) in enumerate([(shift_ref, shift_tile), (frac_ref, frac_tile)])
        for j in range(TILES)
    ]
    for copy in staged:
        copy.start()
    pl.semaphore_wait(barrier, 31)

    def unit(ref, p):
        block, first, many = PIECES[p]
        return ref.at[pl.ds(first, many), block]

    def parked(p):
        _, first, many = PIECES[p]
        return relay_buf.at[pl.ds(first, many), p - PLUS]

    def send(source, target, send_sem, recv_sem, device):
        return pltpu.make_async_remote_copy(
            source, target, send_sem, recv_sem, device_id=device, device_id_type=MESH)

    def direct(p):
        return send(unit(t_ref, p), unit(near_buf, p), first_send.at[p], first_recv.at[p], after)

    def forward(p):
        return send(unit(near_buf, p), unit(far_buf, p), last_send.at[p], last_recv.at[p], after)

    def leg_1(p):
        return send(unit(t_ref, p), parked(p), first_send.at[p], first_recv.at[p], via)

    def leg_2(p):
        return send(parked(p), unit(far_buf, p), middle_send.at[p - PLUS],
                    middle_recv.at[p - PLUS], relayed_to)

    def leg_3(p):
        return send(unit(far_buf, p), unit(near_buf, p), last_send.at[p], last_recv.at[p], ahead)

    tail = pl.ds(COLS - LANES, LANES)
    edge_s = pltpu.make_async_remote_copy(
        shift_ref.at[:, tail], shift_tile.at[0, pl.ds(0, ROWS)], edge_send.at[0], edge_recv.at[0],
        device_id=after, device_id_type=MESH)
    edge_f = pltpu.make_async_remote_copy(
        frac_ref.at[:, tail], frac_tile.at[0, pl.ds(0, ROWS)], edge_send.at[1], edge_recv.at[1],
        device_id=after, device_id_type=MESH)
    edge_s.start()
    edge_f.start()
    for i in range(max(AHEAD, AHEAD_MINUS)):
        if i < AHEAD:
            direct(i).start()
        if i < AHEAD_MINUS:
            leg_1(PLUS + i).start()

    lane = lax.broadcasted_iota(jnp.int32, (TR, LANES), 1)
    zero = jnp.zeros((CR, TR, LANES), jnp.float32)
    work[0] = zero
    work[1] = zero
    work[WIDTH - 1] = zero
    cell = lax.broadcasted_iota(jnp.int32, (COLS, LANES), 0)
    face_lane = lax.broadcasted_iota(jnp.int32, (COLS, LANES), 1)
    face = 2 * (face_lane % 64) + face_lane // 64
    ones_mat[0:COLS, :] = jnp.where(cell < face * BLOCK, 1.0, 0.0).astype(jnp.bfloat16)
    ones_mat[COLS:, :] = jnp.ones((LANES, LANES), jnp.bfloat16)

    for copy in staged:
        copy.wait()
    slot = lax.broadcasted_iota(jnp.int32, (LANES, LANES), 0)
    column = lax.broadcasted_iota(jnp.int32, (LANES, LANES), 1)
    first_hot = jnp.zeros((LANES, LANES), jnp.float32)
    second_hot = first_hot
    code = first_hot
    for j in range(16):
        owner = owner_ref[0, j]
        earlier = jnp.int32(0)
        for i in range(j):
            earlier = earlier + jnp.where(owner_ref[0, i] == owner, 1, 0)
        at = owner * 8 + 2 * earlier
        at_face = source_ref[0, j] + 1
        here = column == (at_face % 2) * 64 + at_face // 2
        label = (parity_ref[0, j] * 32 + place_ref[0, j] + 1).astype(jnp.float32)
        first_hot = jnp.where((slot == at) & here, 1.0, first_hot)
        second_hot = jnp.where((slot == at + 1) & here, 1.0, second_hot)
        code = jnp.where((slot == at + 4) | (slot == at + 5), label, code)
    hots[0] = first_hot.astype(jnp.bfloat16)
    hots[1] = second_hot.astype(jnp.bfloat16)
    codes[...] = code

    edge_s.wait_recv()
    edge_f.wait_recv()
    least = jnp.min(jnp.min(shift_tile[:, 0:ROWS, :], axis=0), axis=1, keepdims=True)
    least_v[...] = jnp.broadcast_to(least, (ROWS, LANES))
    least_copy = pltpu.make_async_copy(least_v, least_s, least_sem)
    least_copy.start()

    def one_row(local, c):
        r = c * CR + local
        low = least_s[r, 0]
        start = OWN * LANES - LANES - 5 - low
        tile = start // LANES
        turn = start % LANES
        piece = []
        for j in range(11):
            piece.append(pltpu.roll(work[tile + j, local], (LANES - turn) % LANES, 1))
        moved = [jnp.where(lane < LANES - turn, piece[j], piece[j + 1]) for j in range(10)]
        cells = [shifted(moved, 5 - i) for i in range(6)]
        gains = []
        for j in range(9):
            n = shift_tile[j, pl.ds(r, TR, stride=0), :]
            f = frac_tile[j, pl.ds(r, TR, stride=0), :]
            offset = n - low
            upwind = cells[0][j]
            before = cells[1][j]
            passed = jnp.zeros((TR, LANES), jnp.float32)
            total = passed
            for step in range(1, 5):
                total = total + cells[step - 1][j]
                hit = offset == step
                upwind = jnp.where(hit, cells[step][j], upwind)
                before = jnp.where(hit, cells[step + 1][j], before)
                passed = jnp.where(hit, total, passed)
            gains.append(passed + f * upwind + (upwind - before) * (f * (1.0 - f) * 0.5))
        back = [pltpu.roll(gain, 1, 1) for gain in gains]
        at_lhs = pl.ds(pl.multiple_of(local * TR, TR), TR)
        for j in range(1, 9):
            advected = cells[0][j] + jnp.where(lane == 0, back[j - 1], back[j]) - gains[j]
            out_ref[r, :, (j - 1) * LANES : j * LANES] = advected
            own = work[OWN + j - 1, local]
            lhs[at_lhs, pl.ds((j - 1) * LANES, LANES)] = own - advected
        whole = jnp.where(lane == LANES - 1, gains[0], 0.0)
        for j in range(PAD, OWN):
            reached = lane >= (OWN - j) * LANES - low
            whole = whole + jnp.where(reached, work[j, local], 0.0)
        lhs[at_lhs, pl.ds(COLS, LANES)] = whole
        return c

    def finish(c):
        for p, piece in enumerate(PIECES):
            if piece[0] == c:
                (forward(p) if p < PLUS else leg_3(p)).wait_recv()
        for j in range(TILES):
            work[PAD + j] = jnp.where(s >= 2, jnp.transpose(far_buf[:, c, j], (1, 0, 2)), 0.0)
            work[PAD + TILES + j] = jnp.where(
                s >= 1, jnp.transpose(near_buf[:, c, j], (1, 0, 2)), 0.0)
            work[OWN + j] = jnp.transpose(own_buf[:, c, j], (1, 0, 2))
        lax.fori_loop(0, CR, one_row, c, unroll=8)
        faces[pl.ds(pl.multiple_of(c * CR * TR, CR * TR), CR * TR), :] = times_hot(
            lhs[...], ones_mat[...], (((1,), (0,)), ((), ())))

    across = (((1,), (1,)), ((), ()))
    half = ROWS // 4 * TR

    def pack(h):
        pairs = faces[2 * h * half : 2 * (h + 1) * half, :].reshape(ROWS // 4, 2, TR, LANES)
        fine = (0.5 * (pairs[:, 0] + pairs[:, 1])).reshape(half, LANES)
        high = fine.astype(jnp.bfloat16)
        rest = fine - high.astype(jnp.float32)
        middle = rest.astype(jnp.bfloat16)
        last = (rest - middle.astype(jnp.float32)).astype(jnp.bfloat16)
        hot = hots[h]
        return sum(
            lax.dot_general(hot, part, across, preferred_element_type=jnp.float32)
            for part in (last, middle, high))

    def pass_on(p):
        direct(p).wait_recv()
        forward(p).start()
        if p + AHEAD < PLUS:
            direct(p).wait_send()
            direct(p + AHEAD).start()

    def first_on(p):
        leg_1(p).wait_recv()
        leg_2(p).start()
        if p + AHEAD_MINUS < len(PIECES):
            leg_1(p).wait_send()
            leg_1(p + AHEAD_MINUS).start()

    def second_on(p):
        leg_2(p).wait_recv()
        leg_3(p).start()

    pass_on(0)
    first_on(5)
    pass_on(1)
    first_on(6)
    pass_on(2)
    first_on(7)
    second_on(5)
    pass_on(3)
    second_on(6)
    pass_on(4)
    second_on(7)
    own_copy.wait()
    least_copy.wait()
    finish(0)
    finish(1)
    finish(2)
    finish(5)
    finish(3)
    codes[...] += pack(0)
    finish(6)
    finish(7)
    finish(4)

    packed = codes[...] + pack(1)
    send_buf[...] = packed.reshape(16, 8, LANES)

    def message(other, other_row, slot_base, k):
        return pltpu.make_async_remote_copy(
            send_buf.at[other], recv_buf.at[slot_base + s], msg_send.at[k], msg_recv,
            device_id=(other, other_row), device_id_type=MESH)

    to_self = pltpu.make_async_copy(send_buf.at[s], recv_buf.at[s], msg_recv)
    to_self.start()
    message(s, partner, 16, 0).start()

    def send_out(step, carry):
        other = (s + step) % 16
        message(other, row, 0, 2 * step).start()
        message(other, partner, 16, 2 * step + 1).start()
        return carry

    for step in FAR_FIRST:
        send_out(step, 0)

    for p in range(len(PIECES)):
        (forward(p) if p < PLUS else leg_3(p)).wait_send()
        if PLUS - AHEAD <= p < PLUS:
            direct(p).wait_send()
        if p >= PLUS:
            leg_2(p).wait_send()
        if p >= len(PIECES) - AHEAD_MINUS:
            leg_1(p).wait_send()
    edge_s.wait_send()
    edge_f.wait_send()

    pltpu.make_async_copy(recv_buf, recv_buf, msg_recv).wait()

    received = recv_buf[...]
    names = pltpu.roll(received, 4, 1).reshape(2 * LANES, LANES)
    received = received.reshape(2 * LANES, LANES)
    part = lax.broadcasted_iota(jnp.int32, (2 * LANES, LANES), 0) % 8
    spot = lax.broadcasted_iota(jnp.int32, (2 * LANES, LANES), 1)
    group = spot % 64 // TILES
    block = 2 * (spot % TILES) + spot // 64
    wanted = jnp.where(group < 4, (row % 2) * 32 + 2 * block + group % 2 + 1, -1).astype(jnp.float32)
    hot = jnp.where((names == wanted) & ((part == group // 2) | (part == group // 2 + 2)), 1.0, 0.0)
    hot = hot.astype(jnp.bfloat16)
    down = (((0,), (0,)), ((), ()))
    sums[...] = times_hot(received, hot, down)
    count = jnp.dot(jnp.ones((TR, 2 * LANES), jnp.bfloat16), hot, preferred_element_type=jnp.float32)

    for side in range(2):
        count_here = count if side == 0 else pltpu.roll(count, LANES - side * TILES, 1)
        for h in range(2):
            base = side * 32 + h * 16
            back = (LANES - (h * 2 + side) * TILES) % LANES

            def fix(k, carry, base=base, back=back, count_here=count_here):
                r = base + k
                sent = sums[pl.ds(pl.multiple_of(k * TR, TR), TR), :]
                sent = pltpu.roll(sent, back, 1) if back else sent
                left = faces[pl.ds(pl.multiple_of(r * TR, TR), TR), :]
                change = 0.5 * (sent - count_here * left)
                for j in range(TILES):
                    turned = pltpu.roll(change, LANES - j, 1) if j else change
                    out_ref[r, :, j * LANES : (j + 1) * LANES] += jnp.where(
                        lane % 64 == 0, turned, 0.0)
                return carry

            lax.fori_loop(0, 16, fix, 0, unroll=16)

    message(s, partner, 16, 0).wait_send()

    def clean_message(step, carry):
        other = (s + step) % 16
        message(other, row, 0, 2 * step).wait_send()
        message(other, partner, 16, 2 * step + 1).wait_send()
        return carry

    lax.fori_loop(1, 16, clean_message, 0)


def per_device(
    tracers, shifts, fractions, record_owner, record_source, record_parity, record_place
):
    tiled = (TR, CHUNKS, TILES, CR, LANES)
    in_tiles = jnp.transpose(tracers.reshape(TR, CHUNKS, CR, TILES, LANES), (0, 1, 3, 2, 4))
    hbm = pl.BlockSpec(memory_space=pltpu.HBM)
    f32 = jnp.float32
    dma = pltpu.SemaphoreType.DMA
    swept = pl.pallas_call(
        sweep_kernel,
        out_shape=jax.ShapeDtypeStruct((ROWS, TR, COLS), f32),
        in_specs=[hbm] * 7,
        out_specs=pl.BlockSpec(memory_space=pltpu.VMEM),
        scratch_shapes=[
            pltpu.SMEM((1, 16), jnp.int32),
            pltpu.SMEM((1, 16), jnp.int32),
            pltpu.SMEM((1, 16), jnp.int32),
            pltpu.SMEM((1, 16), jnp.int32),
            pltpu.VMEM(tiled, f32),
            pltpu.VMEM(tiled, f32),
            pltpu.VMEM(tiled, f32),
            pltpu.VMEM((WIDTH, CR, TR, LANES), f32),
            pltpu.VMEM((TR, MINUS, TILES, CR, LANES), f32),
            pltpu.VMEM((9, ROWS + TR, LANES), jnp.int32),
            pltpu.VMEM((9, ROWS + TR, LANES), f32),
            pltpu.VMEM((ROWS, LANES), jnp.int32),
            pltpu.SMEM((ROWS, LANES), jnp.int32),
            pltpu.VMEM((CR * TR, COLS + LANES), f32),
            pltpu.VMEM((COLS + LANES, LANES), jnp.bfloat16),
            pltpu.VMEM((ROWS * TR, LANES), f32),
            pltpu.VMEM((2, LANES, LANES), jnp.bfloat16),
            pltpu.VMEM((LANES, LANES), f32),
            pltpu.VMEM((LANES, LANES), f32),
            pltpu.VMEM((16, 8, LANES), f32),
            pltpu.VMEM((32, 8, LANES), f32),
            dma, dma((2, TILES)), dma((4,)), dma((2,)), dma((2,)), dma,
            dma((len(PIECES),)), dma((len(PIECES),)), dma((MINUS,)), dma((MINUS,)),
            dma((len(PIECES),)), dma((len(PIECES),)),
            dma((32,)), dma, dma,
        ],
        compiler_params=pltpu.CompilerParams(
            collective_id=0, has_side_effects=True, vmem_limit_bytes=40 << 20),
    )(
        *[pltpu.with_memory_space_constraint(v, pltpu.HBM) for v in (in_tiles, shifts, fractions, record_owner.reshape(1, 16), record_source, record_parity, record_place)]
    )
    return jnp.transpose(swept, (1, 0, 2))


def solution(mesh):
    return jax.shard_map(
        per_device,
        mesh=mesh,
        in_specs=(
            P(None, "rows", "stream"),
            P("rows", "stream"),
            P("rows", "stream"),
            P("rows", "stream", None),
            P("rows", "stream"),
            P("rows", "stream"),
            P("rows", "stream"),
        ),
        out_specs=P(None, "rows", "stream"),
        check_vma=False,
    )
```
